32 devices in a mesh: wide: 16 (over z, y, x), narrow: 2 (over core).
Axes of the slice: x: 2, y: 2, z: 4, core: 2. Of those that a mesh axis runs over, the one named last changes fastest.
Arguments:
- features: float32 [2, 16, 512, 256], P('narrow', 'wide'), may hold values from -6 to 6
- out_grad: float32 [2, 16, 512, 256], P('narrow', 'wide'), may hold values from -0.06629126 to 0.06629126
- bank: float32 [4, 256, 2304], P(None, 'wide'), may hold values from -0.125 to 0.125
- mix_seed: int32 [16, 4], replicated, may hold values from 0 to 255
- style_of: int32 [2], P('narrow'), may hold values from 0 to 15
Outputs:
- bank_grad: float32 [4, 256, 2304], P(None, 'wide')
The draws below stay inside these ranges and needn't reach their ends.
All inputs are finite; a program needn't handle non-finite values.
Results may differ from the reference program's by a relative error of at most 0.0001.
Values sent between devices are 32-bit elements; how exact they have to be, the bound alone decides.
No kernel may reach another device: no remote copies, remote signals or barrier semaphores. Data moves between devices by JAX's collectives and lax.ppermute only.
A program may use at most 64 MiB of HBM per device.

```python
import jax
import jax.numpy as jnp
from jax import lax

C_IN = 256
C_OUT = 256
BANK = 4
STYLES = 16
WIDTH = 512
HEIGHT = 16
SAMPLES = 2


def plant(entries, own_key, low, top_value):
    extent = entries.shape
    spot = [jax.random.randint(jax.random.fold_in(own_key, axis), (), 0, extent[axis]) for axis in range(len(extent))]
    entries = entries.at[tuple(spot)].set(low)
    longest = extent.index(max(extent))
    spot[longest] = (spot[longest] + 1) % extent[longest]
    return entries.at[tuple(spot)].set(top_value)


def strengthened(array, stream_key, source, target, shards_of, factor):
    def block_of(dim):
        return (jnp.arange(array.shape[dim]) // (array.shape[dim] // shards_of)).reshape((-1,) + (1,) * (array.ndim - 1 - dim))

    first = jax.random.permutation(stream_key, shards_of)[block_of(target)]
    second = (block_of(target) + shards_of // 2) % shards_of
    return jnp.where((block_of(source) == first) | (block_of(source) == second), factor * array, array)


def levels(key, shape, split, low, largest):
    level = 1.0
    for dim, blocks in split:
        draws = jax.random.uniform(jax.random.fold_in(jax.random.fold_in(key, 6), dim), (blocks,), jnp.float32, low / len(split), largest / len(split))
        level = level * jnp.repeat(jnp.exp(draws), shape[dim] // blocks).reshape((-1,) + (1,) * (len(shape) - 1 - dim))
    return level


def centred(own_key, extent, spread, most, shards=(), kind=jnp.bfloat16):
    array = jax.random.normal(own_key, extent, jnp.float32) * spread
    if len(shards) > 0:
        array = levels(own_key, extent, shards, -0.22, 0.18) * array
    return jnp.clip(array, min=-most, max=most).astype(kind)


def heavy_noise(key, extent, spread, limit, cuts, heavy, held_as=jnp.bfloat16):
    result = spread * jax.random.normal(key, extent, jnp.float32)
    if cuts:
        result = result * levels(key, extent, cuts, -0.22, 0.18)
    return jnp.clip(strengthened(result, jax.random.fold_in(key, 3), *heavy), -limit, limit).astype(held_as)


def setup_inputs(seed: int = 0) -> dict:
    key_list = jax.random.split(jax.random.key(seed), 6)
    return {
        "features": centred(key_list[0], (SAMPLES, HEIGHT, WIDTH, C_IN), 1.0, 6.0, ((0, 2), (1, 16)), jnp.float32),
        "out_grad": heavy_noise(key_list[1], (SAMPLES, HEIGHT, WIDTH, C_OUT), (1.0 / (HEIGHT * WIDTH) ** 0.5), 0.06629126, ((0, 2), (1, 16)), (1, 3, 16, 2.0), jnp.float32),
        "bank": centred(key_list[2], (BANK, C_OUT, 9 * C_IN), (9 * C_IN) ** -0.5, 0.125, ((1, 16),), jnp.float32),
        "mix_seed": plant(jax.random.randint(key_list[3], (STYLES, BANK), 0, 256), jax.random.fold_in(key_list[3], 1), 0, 255).astype(jnp.int32),
        "style_of": jax.random.randint(key_list[4], (SAMPLES,), 0, STYLES).astype(jnp.int32),
    }


def tap_products(padded, grad_flat, tile_rows, map_width):
    pieces = []
    for row_off in range(3):
        for col_off in range(3):
            window = padded[row_off:row_off + tile_rows, col_off:col_off + map_width]
            window = window.reshape(tile_rows * map_width, window.shape[2])
            pieces.append(lax.dot_general(grad_flat, window, (((0,), (0,)), ((), ())), precision=lax.Precision.HIGHEST, preferred_element_type=jnp.float32))
    return jnp.concatenate(pieces, axis=1)

def demod_back(mixed, kernel_grad):
    scale = lax.rsqrt(lax.optimization_barrier(jnp.sum(mixed * mixed, axis=1, keepdims=True)) + 1e-08)
    inner = lax.optimization_barrier(jnp.sum(mixed * kernel_grad, axis=1, keepdims=True))
    return scale * kernel_grad - scale * scale * scale * mixed * inner

def reference(features, out_grad, bank, mix_seed, style_of):
    mixes = mix_seed[style_of].astype(jnp.float32) / 128.0 + 0.25

    def one_sample(inputs):
        sample_map, sample_out, weights = inputs
        padded = jnp.pad(sample_map, ((1, 1), (1, 1), (0, 0)))
        grad_flat = sample_out.reshape(HEIGHT * WIDTH, C_OUT)
        kernel_grad = tap_products(padded, grad_flat, HEIGHT, WIDTH)
        mixed = jnp.einsum('k,koj->oj', weights, bank, precision=lax.Precision.HIGHEST)
        return demod_back(mixed, kernel_grad)
    sample_grads = lax.map(one_sample, (features, out_grad, mixes))
    return jnp.einsum('sk,soj->koj', mixes, sample_grads, precision=lax.Precision.HIGHEST)
```

```python
import functools

import jax
import jax.numpy as jnp
from jax import lax
from jax.experimental import pallas as pl
from jax.experimental.pallas import tpu as pltpu
from jax.sharding import PartitionSpec as P


F32, BF16 = jnp.float32, jnp.bfloat16
VMEM_SPEC = pl.BlockSpec(memory_space=pltpu.VMEM)
SMEM_SPEC = pl.BlockSpec(memory_space=pltpu.SMEM)


def place():
    me = lax.axis_index("wide")
    return me // 4, me % 4, me % 2, (me // 2) % 2


def call(body, outs, n_in, flops=0, smem=(), scratch=(), name=None):
    specs = [SMEM_SPEC if i in smem else VMEM_SPEC for i in range(n_in)]
    return pl.pallas_call(
        body,
        out_shape=outs,
        in_specs=specs,
        out_specs=jax.tree.map(lambda _: VMEM_SPEC, outs),
        scratch_shapes=list(scratch),
        compiler_params=pltpu.CompilerParams(vmem_limit_bytes=48 * 2**20),
        cost_estimate=pl.CostEstimate(flops=flops, bytes_accessed=2**20, transcendentals=0),
        name=name,
    )


def prep_body(owned, f_ref, g_ref, f_keep, f_send, g_keep, g_send):
    _, _, x, y = place()
    half = f_keep.shape[1]
    f_keep[...] = f_ref[0, 0, :, pl.ds(pl.multiple_of(y * half, half), half)]
    f_send[...] = f_ref[0, 0, :, pl.ds(pl.multiple_of((1 - y) * half, half), half)]
    turned = jnp.transpose(g_ref[0, 0])
    for k in range(turned.shape[0] // (2 * owned)):
        low = turned[2 * k * owned : (2 * k + 1) * owned]
        high = turned[(2 * k + 1) * owned : (2 * k + 2) * owned]
        rows = slice(k * owned, (k + 1) * owned)
        g_keep[rows] = jnp.where(x == 0, low, high)
        g_send[rows] = jnp.where(x == 0, high, low)


def split(v):
    high = v.astype(BF16)
    return high, (v - high.astype(F32)).astype(BF16)


def shifted(g):
    width = g.shape[1]
    at = lax.broadcasted_iota(jnp.int32, g.shape, 1)
    ahead = jnp.where(at == width - 1, 0.0, pltpu.roll(g, width - 1, 1))
    behind = jnp.where(at == 0, 0.0, pltpu.roll(g, 1, 1))
    return split(jnp.concatenate([ahead, g, behind], axis=0))


def product(left_high, left_low, right, half):
    both = jnp.dot(left_high, right, preferred_element_type=F32)
    return (
        both[:, :half]
        + both[:, half:]
        + jnp.dot(left_low, right[:, :half], preferred_element_type=F32)
    )


def main_body(groups, owned, *refs):
    fs, gs = refs[0:5], refs[5:10]
    outs = refs[10 : 10 + groups]
    acc, lh, ll, rt = refs[10 + groups :]
    g, l, x, y = place()
    half = fs[0].shape[1]
    for role in range(5):
        high, low = shifted(gs[role][...])
        lh[role] = high
        ll[role] = low
        high, low = split(fs[role][...])
        rt[role, :, :half] = high
        rt[role, :, half:] = low

    def mul(a, b):
        return product(lh[a], ll[a], rt[b], half)

    own, xn, yn, dg, ex = range(5)
    edge = jnp.where(x == 1, l, 3 ^ l)
    one, two = 1 ^ l, 2 ^ l
    up = jnp.where(x == 0, 2, 0)
    down = 2 - up
    acc[1] = mul(own, own) + mul(xn, xn) + mul(yn, yn) + mul(dg, dg)
    acc[up] = mul(own, xn) + mul(yn, dg) + mul(edge, ex)
    acc[down] = mul(xn, own) + mul(dg, yn) + mul(ex, edge)
    acc[2] += mul(one, two)
    acc[0] += mul(two, one)
    n_out = gs[0].shape[0]
    rows = 2 * owned
    for m in range(groups):
        start = pl.multiple_of((g ^ m) * rows, rows)
        for a in range(3):
            for b in range(3):
                outs[m][3 * a + b] = acc[a, pl.ds(b * n_out + start, rows), :]


def sum_body(owned, *refs):
    parts, (keep, send) = refs[:-2], refs[-2:]
    _, _, _, y = place()
    for t in range(keep.shape[0]):
        total = parts[0][t]
        for part in parts[1:]:
            total = total + part[t]
        low, high = total[:owned], total[owned:]
        keep[t] = jnp.where(y == 0, low, high)
        send[t] = jnp.where(y == 0, high, low)


def final_body(kept_ref, got_ref, bank_ref, seed_ref, style_ref, out_ref):
    _, _, _, y = place()
    samples, taps = kept_ref.shape[:2]
    kinds = bank_ref.shape[0]
    weights, grads = [], []
    for s in range(samples):
        mix = [seed_ref[style_ref[s], k].astype(F32) / 128.0 + 0.25 for k in range(kinds)]
        mixed = mix[0] * bank_ref[0]
        for k in range(1, kinds):
            mixed = mixed + mix[k] * bank_ref[k]
        pieces = []
        for t in range(taps):
            kept, got = kept_ref[s, t], got_ref[s, t]
            pieces += [jnp.where(y == 0, kept, got), jnp.where(y == 0, got, kept)]
        grad = jnp.concatenate(pieces, axis=1)
        scale = lax.rsqrt(jnp.sum(mixed * mixed, axis=1, keepdims=True) + 1e-08)
        inner = jnp.sum(mixed * grad, axis=1, keepdims=True)
        grads.append(scale * grad - (scale * scale * scale * inner) * mixed)
        weights.append(mix)
    for k in range(kinds):
        total = weights[0][k] * grads[0]
        for s in range(1, samples):
            total = total + weights[s][k] * grads[s]
        out_ref[k] = total


def send(value, pairs):
    return lax.ppermute(value, "wide", pairs)


def local(features, out_grad, bank, mix_seed, style_of):
    size = lax.axis_size("wide")
    groups = size // 4
    _, _, map_width, in_channels = features.shape
    out_channels = out_grad.shape[3]
    owned = bank.shape[1]
    half_in, half_out = in_channels // 2, out_channels // 2
    everyone = range(size)
    over_x = [(i, i ^ 1) for i in everyone]
    over_y = [(i, i ^ 2) for i in everyone]
    outward = [(i, i + 4 if i % 2 else i - 4) for i in everyone]
    outward = [(i, j) for i, j in outward if 0 <= j < size]

    styles = lax.all_gather(style_of, "narrow", axis=0, tiled=True)
    f_shape = jax.ShapeDtypeStruct((map_width, half_in), F32)
    g_shape = jax.ShapeDtypeStruct((half_out, map_width), F32)
    f_keep, f_send, g_keep, g_send = call(
        functools.partial(prep_body, owned), (f_shape, f_shape, g_shape, g_shape), 2, name="prep"
    )(features, out_grad)

    g_xn = send(g_send, over_x)
    f_yn = send(f_send, over_y)
    f_xn = send(f_keep, over_x)
    g_yn = send(g_keep, over_y)
    f_dg = send(f_yn, over_x)
    g_dg = send(g_xn, over_y)
    me = lax.axis_index("wide")
    same = (me % 2) == ((me // 2) % 2)
    f_ex = send(jnp.where(same, f_keep, f_yn), outward)
    g_ex = send(jnp.where(same, g_keep, g_yn), outward)

    block = jax.ShapeDtypeStruct((9, 2 * owned, half_in), F32)
    blocks = call(
        functools.partial(main_body, groups, owned),
        [block] * groups,
        10,
        flops=2 * 3 * 12 * 3 * half_out * half_in * map_width,
        scratch=(
            pltpu.VMEM((3, 3 * half_out, half_in), F32),
            pltpu.VMEM((5, 3 * half_out, map_width), BF16),
            pltpu.VMEM((5, 3 * half_out, map_width), BF16),
            pltpu.VMEM((5, map_width, 2 * half_in), BF16),
        ),
        name="main",
    )(f_keep, f_xn, f_yn, f_dg, f_ex, g_keep, g_xn, g_yn, g_dg, g_ex)
    parts = [blocks[0]] + [
        send(blocks[m], [(i, i ^ (4 * m)) for i in everyone]) for m in range(1, groups)
    ]
    piece = jax.ShapeDtypeStruct((9, owned, half_in), F32)
    keep, give = call(functools.partial(sum_body, owned), (piece, piece), groups, name="sum")(*parts)
    got = send(give, over_y)
    every_keep = lax.all_gather(keep[None], "narrow", axis=0, tiled=True)
    every_got = lax.all_gather(got[None], "narrow", axis=0, tiled=True)
    return call(
        final_body,
        jax.ShapeDtypeStruct(bank.shape, F32),
        5,
        smem=(3, 4),
        name="final",
    )(every_keep, every_got, bank, mix_seed, styles)


def solution(mesh):
    placed = (
        P("narrow", "wide", None, None),
        P("narrow", "wide", None, None),
        P(None, "wide", None),
        P(),
        P("narrow"),
    )
    return jax.shard_map(
        local, mesh=mesh, in_specs=placed, out_specs=P(None, "wide", None), check_vma=False
    )
```

```python
import functools

import jax
import jax.numpy as jnp
from jax import lax
from jax.experimental import pallas as pl
from jax.experimental.pallas import tpu as pltpu
from jax.sharding import PartitionSpec as P


F32, BF16 = jnp.float32, jnp.bfloat16
VMEM_SPEC = pl.BlockSpec(memory_space=pltpu.VMEM)
SMEM_SPEC = pl.BlockSpec(memory_space=pltpu.SMEM)
ANY_SPEC = pl.BlockSpec(memory_space=pl.ANY)


def place():
    me = lax.axis_index("wide")
    return me // 4, me % 4, me % 2, (me // 2) % 2


def call(body, outs, ins, out_specs=None, flops=0, scratch=(), alias=None, limit=40 * 2**20):
    return pl.pallas_call(
        body,
        out_shape=outs,
        in_specs=[{"v": VMEM_SPEC, "s": SMEM_SPEC, "a": ANY_SPEC}[i] for i in ins],
        out_specs=jax.tree.map(lambda _: VMEM_SPEC, outs) if out_specs is None else out_specs,
        scratch_shapes=list(scratch),
        input_output_aliases=alias or {},
        compiler_params=pltpu.CompilerParams(vmem_limit_bytes=limit),
        cost_estimate=pl.CostEstimate(flops=flops, bytes_accessed=2**20, transcendentals=0),
    )


def features_body(f_ref, f_keep, f_send):
    _, _, _, y = place()
    half = f_keep.shape[1]
    f_send[...] = f_ref[0, 0, :, pl.ds(pl.multiple_of((1 - y) * half, half), half)]
    f_keep[...] = f_ref[0, 0, :, pl.ds(pl.multiple_of(y * half, half), half)]


def grads_body(owned, g_ref, seed_ref, style_ref, g_keep, g_send, mix):
    _, _, x, _ = place()
    at = lax.broadcasted_iota(jnp.int32, mix.shape, 0)
    tile = jnp.zeros(mix.shape, F32)
    for k in range(seed_ref.shape[0]):
        weight = seed_ref[k, style_ref[0]].astype(F32) / 128.0 + 0.25
        tile = jnp.where(at == k, weight, tile)
    mix[...] = tile
    turned = jnp.transpose(g_ref[0, 0])
    for k in range(turned.shape[0] // (2 * owned)):
        low = turned[2 * k * owned : (2 * k + 1) * owned]
        high = turned[(2 * k + 1) * owned : (2 * k + 2) * owned]
        rows = slice(k * owned, (k + 1) * owned)
        g_keep[rows] = jnp.where(x == 0, low, high)
        g_send[rows] = jnp.where(x == 0, high, low)


def mix_body(every_ref, bank_ref, f_in, g_in, mixed_ref, scale_ref, f_out, g_out):
    samples, kinds = every_ref.shape[0], bank_ref.shape[0]
    for s in range(samples):
        mixed = every_ref[s, 0:1, 0:1] * bank_ref[0]
        for k in range(1, kinds):
            mixed = mixed + every_ref[s, k : k + 1, 0:1] * bank_ref[k]
        mixed_ref[s] = mixed
        scale = lax.rsqrt(jnp.sum(mixed * mixed, axis=1, keepdims=True) + 1e-08)
        scale_ref[s] = jnp.broadcast_to(scale, scale_ref.shape[1:])


def split(v):
    high = v.astype(BF16)
    return high, (v - high.astype(F32)).astype(BF16)


def shifted(g):
    width = g.shape[1]
    at = lax.broadcasted_iota(jnp.int32, g.shape, 1)
    ahead = jnp.where(at == width - 1, 0.0, pltpu.roll(g, width - 1, 1))
    behind = jnp.where(at == 0, 0.0, pltpu.roll(g, 1, 1))
    return split(jnp.concatenate([ahead, g, behind], axis=0))


def product(left_high, left_low, right, half):
    both = jnp.dot(left_high, right, preferred_element_type=F32)
    return (
        both[:, :half]
        + both[:, half:]
        + jnp.dot(left_low, right[:, :half], preferred_element_type=F32)
    )


def operands(f, g, lh, ll, rt):
    half = f.shape[1]
    lh[...], ll[...] = shifted(g[...])
    high, low = split(f[...])
    rt[:, :half] = high
    rt[:, half:] = low


def near_body(*refs):
    fs, gs, acc, lh, ll, rt = refs[0:3], refs[3:6], *refs[6:]
    _, _, x, _ = place()
    half = fs[0].shape[1]
    for role in range(3):
        operands(fs[role], gs[role], lh.at[role], ll.at[role], rt.at[role])

    def mul(a, b):
        return product(lh[a], ll[a], rt[b], half)

    up = jnp.where(x == 0, 2, 0)
    acc[1] = mul(0, 0) + mul(1, 1) + mul(2, 2)
    acc[up] = mul(0, 1)
    acc[2 - up] = mul(1, 0)


def far_body(f, g, acc_in, lh, ll, rt, acc, lh_far, ll_far, rt_far):
    _, _, x, y = place()
    half = f.shape[1]
    operands(f, g, lh_far, ll_far, rt_far)
    far = (lh_far, ll_far, rt_far)
    own, xn, yn = [(lh.at[i], ll.at[i], rt.at[i]) for i in range(3)]

    def mul(a, b):
        return product(a[0][...], a[1][...], b[2][...], half)

    up = jnp.where(x == 0, 2, 0)
    acc[1] = acc_in[1] + mul(far, far)
    acc[up] = acc_in[up] + mul(yn, far)
    acc[2 - up] = acc_in[2 - up] + mul(far, yn)
    onward = jnp.where(y == 0, 2, 0)

    def middle(a, b):
        acc[onward] += mul(a, b)
        acc[2 - onward] += mul(b, a)

    pl.when(x == y)(lambda: middle(xn, yn))
    pl.when(x != y)(lambda: middle(own, far))


def edge_body(groups, owned, *refs):
    fe, ge, acc_in, lh, ll, rt, lh_far, ll_far, rt_far = refs[:9]
    outs, acc, lh_ex, ll_ex, rt_ex = refs[9:-4], *refs[-4:]
    group, _, x, y = place()
    half = fe.shape[1]
    operands(fe, ge, lh_ex, ll_ex, rt_ex)
    up = jnp.where(x == 0, 2, 0)
    acc[1] = acc_in[1]

    def outer(lh_in, ll_in, rt_in):
        acc[up] = acc_in[up] + product(lh_in[...], ll_in[...], rt_ex[...], half)
        acc[2 - up] = acc_in[2 - up] + product(lh_ex[...], ll_ex[...], rt_in[...], half)

    pl.when(x == y)(lambda: outer(lh_far, ll_far, rt_far))
    pl.when(x != y)(lambda: outer(lh.at[1], ll.at[1], rt.at[1]))
    n_out = ge.shape[0]
    rows = 2 * owned
    for m in range(groups):
        start = pl.multiple_of((group ^ m) * rows, rows)
        for a in range(3):
            for b in range(3):
                both = acc[a, pl.ds(b * n_out + start, rows), :]
                low, high = both[:owned], both[owned:]
                outs[2 * m][3 * a + b] = jnp.where(y == 0, low, high)
                outs[2 * m + 1][3 * a + b] = jnp.where(y == 0, high, low)


def sum_body(*refs):
    parts, out = refs[:-1], refs[-1]
    taps = parts[0].shape[0]
    for d in range(2):
        for t in range(taps):
            total = parts[d][t]
            for part in parts[d + 2 :: 2]:
                total = total + part[t]
            out[0, d * taps + t] = total


def final_body(sums_ref, every_ref, mixed_ref, scale_ref, out_ref, held, sem):
    _, _, _, y = place()
    samples, taps = sums_ref.shape[0], sums_ref.shape[1] // 2
    kinds = held.shape[0]
    grads = []
    for s in range(samples):
        pieces = []
        for t in range(taps):
            kept, got = sums_ref[s, t], sums_ref[s, taps + t]
            pieces += [jnp.where(y == 0, kept, got), jnp.where(y == 0, got, kept)]
        grad = jnp.concatenate(pieces, axis=1)
        mixed, scale = mixed_ref[s], scale_ref[s, :, 0:1]
        inner = jnp.sum(mixed * grad, axis=1, keepdims=True)
        grads.append(scale * grad - (scale * scale * scale * inner) * mixed)
    copies = []
    for k in range(kinds):
        total = every_ref[0, k : k + 1, 0:1] * grads[0]
        for s in range(1, samples):
            total = total + every_ref[s, k : k + 1, 0:1] * grads[s]
        held[k] = total
        copies.append(pltpu.make_async_copy(held.at[k], out_ref.at[k], sem.at[k]))
        copies[-1].start()
    for copy in copies:
        copy.wait()


def send(value, pairs):
    return lax.ppermute(value, "wide", pairs)


def local(features, out_grad, bank, mix_seed, style_of):
    size = lax.axis_size("wide")
    groups = size // 4
    _, _, map_width, in_channels = features.shape
    out_channels = out_grad.shape[3]
    owned = bank.shape[1]
    half_in, half_out = in_channels // 2, out_channels // 2
    everyone = range(size)
    over_x = [(i, i ^ 1) for i in everyone]
    over_y = [(i, i ^ 2) for i in everyone]
    outward = [(i, i + 4 if i % 2 else i - 4) for i in everyone]
    outward = [(i, j) for i, j in outward if 0 <= j < size]

    def shape(*dims, dtype=F32):
        return jax.ShapeDtypeStruct(dims, dtype)

    f_shape, g_shape = shape(map_width, half_in), shape(half_out, map_width)
    mix_shape = shape(owned, 128)
    f_keep, f_send = call(features_body, (f_shape, f_shape), "v")(features)
    g_keep, g_send, mix = call(
        functools.partial(grads_body, owned), (g_shape, g_shape, mix_shape), "vss"
    )(out_grad, mix_seed.T, style_of)

    f_yn = send(f_send, over_y)
    g_xn = send(g_send, over_x)
    every_mix = lax.all_gather(mix[None], "narrow", axis=0, tiled=True)
    samples = every_mix.shape[0]
    mixed, scale, f_keep, g_keep = call(
        mix_body,
        (shape(samples, *bank.shape[1:]), shape(samples, owned, 128), f_shape, g_shape),
        "vvaa",
        (VMEM_SPEC, VMEM_SPEC, ANY_SPEC, ANY_SPEC),
        alias={2: 2, 3: 3},
    )(every_mix, bank, f_keep, g_keep)
    f_xn = send(f_keep, over_x)
    g_yn = send(g_keep, over_y)
    f_dg = send(f_yn, over_x)
    g_dg = send(g_xn, over_y)
    me = lax.axis_index("wide")
    same = (me % 2) == ((me // 2) % 2)
    f_ex = send(jnp.where(same, f_keep, f_yn), outward)
    g_ex = send(jnp.where(same, g_keep, g_yn), outward)

    pair = 2 * 3 * 3 * half_out * half_in * map_width
    sums = shape(3, 3 * half_out, half_in)
    left = shape(3 * half_out, map_width, dtype=BF16)
    right = shape(map_width, 2 * half_in, dtype=BF16)
    lefts = shape(3, *left.shape, dtype=BF16)
    rights = shape(3, *right.shape, dtype=BF16)
    acc, *near = call(near_body, (sums, lefts, lefts, rights), "v" * 6, flops=5 * pair)(
        f_keep, f_xn, f_yn, g_keep, g_xn, g_yn
    )
    acc, *far = call(far_body, (sums, left, left, right), "v" * 6, flops=5 * pair)(
        f_dg, g_dg, acc, *near
    )
    piece = shape(9, owned, half_in)
    blocks = call(
        functools.partial(edge_body, groups, owned),
        [piece] * (2 * groups),
        "v" * 9,
        flops=2 * pair,
        scratch=[pltpu.VMEM(a.shape, a.dtype) for a in (sums, left, left, right)],
    )(f_ex, g_ex, acc, *near, *far)
    parts = [blocks[0]] + [
        send(blocks[n], [(i, i ^ (2 * n)) for i in everyone])
        for n in range(1, 2 * groups)
    ]
    own_sums = call(sum_body, shape(1, 18, owned, half_in), "v" * (2 * groups))(
        *parts
    )
    every_sum = lax.all_gather(own_sums, "narrow", axis=0, tiled=True)
    return call(
        final_body,
        shape(*bank.shape),
        "vvvv",
        ANY_SPEC,
        scratch=(pltpu.VMEM(bank.shape, F32), pltpu.SemaphoreType.DMA((bank.shape[0],))),
    )(every_sum, every_mix, mixed, scale)


def solution(mesh):
    placed = (
        P("narrow", "wide", None, None),
        P("narrow", "wide", None, None),
        P(None, "wide", None),
        P(),
        P("narrow"),
    )
    return jax.shard_map(
        local, mesh=mesh, in_specs=placed, out_specs=P(None, "wide", None), check_vma=False
    )
```

```python
import functools

import jax
import jax.numpy as jnp
from jax import lax
from jax.experimental import pallas as pl
from jax.experimental.pallas import tpu as pltpu
from jax.sharding import PartitionSpec as P


F32, BF16 = jnp.float32, jnp.bfloat16
VMEM_SPEC = pl.BlockSpec(memory_space=pltpu.VMEM)
SMEM_SPEC = pl.BlockSpec(memory_space=pltpu.SMEM)
ANY_SPEC = pl.BlockSpec(memory_space=pl.ANY)


def place():
    me = lax.axis_index("wide")
    return me // 4, me % 4, me % 2, (me // 2) % 2


def call(body, outs, ins, out_specs=None, flops=0, scratch=(), alias=None, limit=40 * 2**20):
    return pl.pallas_call(
        body,
        out_shape=outs,
        in_specs=[{"v": VMEM_SPEC, "s": SMEM_SPEC, "a": ANY_SPEC}[i] for i in ins],
        out_specs=jax.tree.map(lambda _: VMEM_SPEC, outs) if out_specs is None else out_specs,
        scratch_shapes=list(scratch),
        input_output_aliases=alias or {},
        compiler_params=pltpu.CompilerParams(vmem_limit_bytes=limit),
        cost_estimate=pl.CostEstimate(flops=flops, bytes_accessed=2**20, transcendentals=0),
    )


def features_body(f_ref, f_keep, f_send):
    _, _, _, y = place()
    half = f_keep.shape[1]
    f_send[...] = f_ref[0, 0, :, pl.ds(pl.multiple_of((1 - y) * half, half), half)]
    f_keep[...] = f_ref[0, 0, :, pl.ds(pl.multiple_of(y * half, half), half)]


def weights_body(seed_ref, style_ref, after_ref, mix):
    at = lax.broadcasted_iota(jnp.int32, mix.shape, 0)
    tile = jnp.zeros(mix.shape, F32)
    for k in range(seed_ref.shape[0]):
        weight = seed_ref[k, style_ref[0]].astype(F32) / 128.0 + 0.25
        tile = jnp.where(at == k, weight, tile)
    mix[...] = tile


def grads_body(owned, g_ref, g_keep, g_send):
    _, _, x, _ = place()
    turned = jnp.transpose(g_ref[0, 0])
    for k in range(turned.shape[0] // (2 * owned)):
        low = turned[2 * k * owned : (2 * k + 1) * owned]
        high = turned[(2 * k + 1) * owned : (2 * k + 2) * owned]
        rows = slice(k * owned, (k + 1) * owned)
        g_keep[rows] = jnp.where(x == 0, low, high)
        g_send[rows] = jnp.where(x == 0, high, low)


def mix_body(every_ref, bank_ref, f_in, g_in, mixed_ref, scale_ref, f_out, g_out):
    samples, kinds = every_ref.shape[0], bank_ref.shape[0]
    for s in range(samples):
        mixed = every_ref[s, 0:1, 0:1] * bank_ref[0]
        for k in range(1, kinds):
            mixed = mixed + every_ref[s, k : k + 1, 0:1] * bank_ref[k]
        mixed_ref[s] = mixed
        scale = lax.rsqrt(jnp.sum(mixed * mixed, axis=1, keepdims=True) + 1e-08)
        scale_ref[s] = jnp.broadcast_to(scale, scale_ref.shape[1:])


def split(v):
    high = v.astype(BF16)
    return high, (v - high.astype(F32)).astype(BF16)


def shifted(g):
    width = g.shape[1]
    at = lax.broadcasted_iota(jnp.int32, g.shape, 1)
    ahead = jnp.where(at == width - 1, 0.0, pltpu.roll(g, width - 1, 1))
    behind = jnp.where(at == 0, 0.0, pltpu.roll(g, 1, 1))
    return split(jnp.concatenate([ahead, g, behind], axis=0))


def product(left_high, left_low, right, half):
    both = jnp.dot(left_high, right, preferred_element_type=F32)
    return (
        both[:, :half]
        + both[:, half:]
        + jnp.dot(left_low, right[:, :half], preferred_element_type=F32)
    )


def operands(f, g, lh, ll, rt):
    half = f.shape[1]
    lh[...], ll[...] = shifted(g[...])
    high, low = split(f[...])
    rt[:, :half] = high
    rt[:, half:] = low


def near_body(*refs):
    fs, gs, acc, lh, ll, rt = refs[0:3], refs[3:6], *refs[6:]
    _, _, x, _ = place()
    half = fs[0].shape[1]
    for role in range(3):
        operands(fs[role], gs[role], lh.at[role], ll.at[role], rt.at[role])

    def mul(a, b):
        return product(lh[a], ll[a], rt[b], half)

    up = jnp.where(x == 0, 2, 0)
    acc[1] = mul(0, 0) + mul(1, 1) + mul(2, 2)
    acc[up] = mul(0, 1)
    acc[2 - up] = mul(1, 0)


def far_body(f, g, acc_in, lh, ll, rt, acc, lh_far, ll_far, rt_far):
    _, _, x, y = place()
    half = f.shape[1]
    operands(f, g, lh_far, ll_far, rt_far)
    far = (lh_far, ll_far, rt_far)
    own, xn, yn = [(lh.at[i], ll.at[i], rt.at[i]) for i in range(3)]

    def mul(a, b):
        return product(a[0][...], a[1][...], b[2][...], half)

    up = jnp.where(x == 0, 2, 0)
    acc[1] = acc_in[1] + mul(far, far)
    acc[up] = acc_in[up] + mul(yn, far)
    acc[2 - up] = acc_in[2 - up] + mul(far, yn)
    onward = jnp.where(y == 0, 2, 0)

    def middle(a, b):
        acc[onward] += mul(a, b)
        acc[2 - onward] += mul(b, a)

    pl.when(x == y)(lambda: middle(xn, yn))
    pl.when(x != y)(lambda: middle(own, far))


def edge_body(groups, owned, *refs):
    fe, ge, acc_in, lh, ll, rt, lh_far, ll_far, rt_far = refs[:9]
    outs, acc, lh_ex, ll_ex, rt_ex = refs[9:-4], *refs[-4:]
    group, _, x, y = place()
    half = fe.shape[1]
    operands(fe, ge, lh_ex, ll_ex, rt_ex)

    @pl.when(group == jnp.where(x == 1, 0, groups - 1))
    def _():
        lh_ex[...] = jnp.zeros_like(lh_ex)
        ll_ex[...] = jnp.zeros_like(ll_ex)
        rt_ex[...] = jnp.zeros_like(rt_ex)

    up = jnp.where(x == 0, 2, 0)
    acc[1] = acc_in[1]

    def outer(lh_in, ll_in, rt_in):
        acc[up] = acc_in[up] + product(lh_in[...], ll_in[...], rt_ex[...], half)
        acc[2 - up] = acc_in[2 - up] + product(lh_ex[...], ll_ex[...], rt_in[...], half)

    pl.when(x == y)(lambda: outer(lh_far, ll_far, rt_far))
    pl.when(x != y)(lambda: outer(lh.at[1], ll.at[1], rt.at[1]))
    n_out = ge.shape[0]
    rows = 2 * owned
    for m in range(groups):
        start = pl.multiple_of((group ^ m) * rows, rows)
        for a in range(3):
            for b in range(3):
                both = acc[a, pl.ds(b * n_out + start, rows), :]
                low, high = both[:owned], both[owned:]
                outs[2 * m][3 * a + b] = jnp.where(y == 0, low, high)
                outs[2 * m + 1][3 * a + b] = jnp.where(y == 0, high, low)


def sum_body(*refs):
    parts, out = refs[:-1], refs[-1]
    taps = parts[0].shape[0]
    for d in range(2):
        for t in range(taps):
            total = parts[d][t]
            for part in parts[d + 2 :: 2]:
                total = total + part[t]
            out[0, d * taps + t] = total


def final_body(sums_ref, every_ref, mixed_ref, scale_ref, out_ref, held, sem):
    _, _, _, y = place()
    samples, taps = sums_ref.shape[0], sums_ref.shape[1] // 2
    kinds = held.shape[0]
    grads = []
    for s in range(samples):
        pieces = []
        for t in range(taps):
            kept, got = sums_ref[s, t], sums_ref[s, taps + t]
            pieces += [jnp.where(y == 0, kept, got), jnp.where(y == 0, got, kept)]
        grad = jnp.concatenate(pieces, axis=1)
        mixed, scale = mixed_ref[s], scale_ref[s, :, 0:1]
        inner = jnp.sum(mixed * grad, axis=1, keepdims=True)
        grads.append(scale * grad - (scale * scale * scale * inner) * mixed)
    copies = []
    for k in range(kinds):
        total = every_ref[0, k : k + 1, 0:1] * grads[0]
        for s in range(1, samples):
            total = total + every_ref[s, k : k + 1, 0:1] * grads[s]
        held[k] = total
        copies.append(pltpu.make_async_copy(held.at[k], out_ref.at[k], sem.at[k]))
        copies[-1].start()
    for copy in copies:
        copy.wait()


def send(value, pairs):
    return lax.ppermute(value, "wide", pairs)


def local(features, out_grad, bank, mix_seed, style_of):
    size = lax.axis_size("wide")
    groups = size // 4
    _, _, map_width, in_channels = features.shape
    out_channels = out_grad.shape[3]
    owned = bank.shape[1]
    half_in, half_out = in_channels // 2, out_channels // 2
    everyone = range(size)
    over_x = [(i, i ^ 1) for i in everyone]
    over_y = [(i, i ^ 2) for i in everyone]
    outward = [(i, (i + 4 if i % 2 else i - 4) % size) for i in everyone]

    def shape(*dims, dtype=F32):
        return jax.ShapeDtypeStruct(dims, dtype)

    f_shape, g_shape = shape(map_width, half_in), shape(half_out, map_width)
    mix_shape = shape(owned, 128)
    f_keep, f_send = call(features_body, (f_shape, f_shape), "v", flops=2 * 10**9)(features)
    g_keep, g_send = call(functools.partial(grads_body, owned), (g_shape, g_shape), "v")(out_grad)
    mix = call(weights_body, mix_shape, "ssa")(mix_seed.T, style_of, g_send)

    f_yn = send(f_send, over_y)
    g_xn = send(g_send, over_x)
    every_mix = lax.all_gather(mix[None], "narrow", axis=0, tiled=True)
    samples = every_mix.shape[0]
    mixed, scale, f_keep, g_keep = call(
        mix_body,
        (shape(samples, *bank.shape[1:]), shape(samples, owned, 128), f_shape, g_shape),
        "vvaa",
        (VMEM_SPEC, VMEM_SPEC, ANY_SPEC, ANY_SPEC),
        alias={2: 2, 3: 3},
    )(every_mix, bank, f_keep, g_keep)
    f_xn = send(f_keep, over_x)
    g_yn = send(g_keep, over_y)
    f_dg = send(f_yn, over_x)
    g_dg = send(g_xn, over_y)
    me = lax.axis_index("wide")
    same = (me % 2) == ((me // 2) % 2)
    f_ex = send(jnp.where(same, f_keep, f_yn), outward)
    g_ex = send(jnp.where(same, g_keep, g_yn), outward)

    pair = 2 * 3 * 3 * half_out * half_in * map_width
    sums = shape(3, 3 * half_out, half_in)
    left = shape(3 * half_out, map_width, dtype=BF16)
    right = shape(map_width, 2 * half_in, dtype=BF16)
    lefts = shape(3, *left.shape, dtype=BF16)
    rights = shape(3, *right.shape, dtype=BF16)
    acc, *near = call(near_body, (sums, lefts, lefts, rights), "v" * 6, flops=5 * pair)(
        f_keep, f_xn, f_yn, g_keep, g_xn, g_yn
    )
    acc, *far = call(far_body, (sums, left, left, right), "v" * 6, flops=5 * pair)(
        f_dg, g_dg, acc, *near
    )
    piece = shape(9, owned, half_in)
    blocks = call(
        functools.partial(edge_body, groups, owned),
        [piece] * (2 * groups),
        "v" * 9,
        flops=2 * pair,
        scratch=[pltpu.VMEM(a.shape, a.dtype) for a in (sums, left, left, right)],
    )(f_ex, g_ex, acc, *near, *far)
    parts = [blocks[0]] + [
        send(blocks[n], [(i, i ^ (2 * n)) for i in everyone])
        for n in range(1, 2 * groups)
    ]
    own_sums = call(sum_body, shape(1, 18, owned, half_in), "v" * (2 * groups))(
        *parts
    )
    every_sum = lax.all_gather(own_sums, "narrow", axis=0, tiled=True)
    return call(
        final_body,
        shape(*bank.shape),
        "vvvv",
        ANY_SPEC,
        scratch=(pltpu.VMEM(bank.shape, F32), pltpu.SemaphoreType.DMA((bank.shape[0],))),
    )(every_sum, every_mix, mixed, scale)


def solution(mesh):
    placed = (
        P("narrow", "wide", None, None),
        P("narrow", "wide", None, None),
        P(None, "wide", None),
        P(),
        P("narrow"),
    )
    return jax.shard_map(
        local, mesh=mesh, in_specs=placed, out_specs=P(None, "wide", None), check_vma=False
    )
```

```python
import functools

import jax
import jax.numpy as jnp
from jax import lax
from jax.experimental import pallas as pl
from jax.experimental.pallas import tpu as pltpu
from jax.sharding import PartitionSpec as P


F32, BF16 = jnp.float32, jnp.bfloat16
VMEM_SPEC = pl.BlockSpec(memory_space=pltpu.VMEM)
SMEM_SPEC = pl.BlockSpec(memory_space=pltpu.SMEM)
ANY_SPEC = pl.BlockSpec(memory_space=pl.ANY)


def place():
    me = lax.axis_index("wide")
    return me // 4, me % 4, me % 2, (me // 2) % 2


def call(body, outs, ins, out_specs=None, flops=0, scratch=(), alias=None, limit=40 * 2**20):
    return pl.pallas_call(
        body,
        out_shape=outs,
        in_specs=[{"v": VMEM_SPEC, "s": SMEM_SPEC, "a": ANY_SPEC}[i] for i in ins],
        out_specs=jax.tree.map(lambda _: VMEM_SPEC, outs) if out_specs is None else out_specs,
        scratch_shapes=list(scratch),
        input_output_aliases=alias or {},
        compiler_params=pltpu.CompilerParams(vmem_limit_bytes=limit),
        cost_estimate=pl.CostEstimate(flops=flops, bytes_accessed=2**20, transcendentals=0),
    )


def features_body(f_ref, f_keep, f_send):
    _, _, _, y = place()
    half = f_keep.shape[1]
    f_send[...] = f_ref[0, 0, :, pl.ds(pl.multiple_of((1 - y) * half, half), half)]
    f_keep[...] = f_ref[0, 0, :, pl.ds(pl.multiple_of(y * half, half), half)]


def weights_body(seed_ref, style_ref, after_ref, mix):
    at = lax.broadcasted_iota(jnp.int32, mix.shape, 0)
    tile = jnp.zeros(mix.shape, F32)
    for k in range(seed_ref.shape[0]):
        weight = seed_ref[k, style_ref[0]].astype(F32) / 128.0 + 0.25
        tile = jnp.where(at == k, weight, tile)
    mix[...] = tile


def grads_body(owned, g_ref, g_keep, g_send):
    _, _, x, _ = place()
    turned = jnp.transpose(g_ref[0, 0])
    for k in range(turned.shape[0] // (2 * owned)):
        low = turned[2 * k * owned : (2 * k + 1) * owned]
        high = turned[(2 * k + 1) * owned : (2 * k + 2) * owned]
        rows = slice(k * owned, (k + 1) * owned)
        g_keep[rows] = jnp.where(x == 0, low, high)
        g_send[rows] = jnp.where(x == 0, high, low)


def mix_body(every_ref, bank_ref, f_in, g_in, mixed_ref, scale_ref, f_out, g_out):
    samples, kinds = every_ref.shape[0], bank_ref.shape[0]
    for s in range(samples):
        mixed = every_ref[s, 0:1, 0:1] * bank_ref[0]
        for k in range(1, kinds):
            mixed = mixed + every_ref[s, k : k + 1, 0:1] * bank_ref[k]
        mixed_ref[s] = mixed
        scale = lax.rsqrt(jnp.sum(mixed * mixed, axis=1, keepdims=True) + 1e-08)
        scale_ref[s] = jnp.broadcast_to(scale, scale_ref.shape[1:])


def split(v):
    high = v.astype(BF16)
    return high, (v - high.astype(F32)).astype(BF16)


def shifted(g):
    width = g.shape[1]
    at = lax.broadcasted_iota(jnp.int32, g.shape, 1)
    ahead = jnp.where(at == width - 1, 0.0, pltpu.roll(g, width - 1, 1))
    behind = jnp.where(at == 0, 0.0, pltpu.roll(g, 1, 1))
    return split(jnp.concatenate([ahead, g, behind], axis=0))


def product(left_high, left_low, right, half):
    both = jnp.dot(left_high, right, preferred_element_type=F32)
    return (
        both[:, :half]
        + both[:, half:]
        + jnp.dot(left_low, right[:, :half], preferred_element_type=F32)
    )


def left(g, high, low):
    high[...], low[...] = shifted(g[...])


def right(f, out):
    half = f.shape[1]
    high, low = split(f[...])
    out[:, :half] = high
    out[:, half:] = low


def mul(lefts, role, rights, other):
    half = rights.shape[2] // 2
    return product(lefts[0][role], lefts[1][role], rights[other], half)


def first_body(f_own, f_yn, g_own, g_xn, mid, side, lh, ll, rt):
    _, _, x, y = place()
    left(g_own, lh.at[0], ll.at[0])
    left(g_xn, lh.at[1], ll.at[1])
    right(f_own, rt.at[0])
    right(f_yn, rt.at[1])
    lefts = (lh, ll)
    mid[...] = mul(lefts, 0, rt, 0)
    side[x] = mul(lefts, 1, rt, 0)
    side[1 - x] = jnp.zeros(side.shape[1:], F32)

    @pl.when(x == y)
    def _():
        side[1 - y] += mul(lefts, 1, rt, 1)


def near_body(groups, f_xn, g_yn, f_even, f_odd, mid_in, side_in, lh, ll, rt, mid, side, lh_yn, ll_yn, rt_more):
    group, _, x, y = place()
    left(g_yn, lh_yn.at[0], ll_yn.at[0])
    right(f_xn, rt_more.at[0])
    from_even = group % 2 == x
    pl.when(from_even)(lambda: right(f_even, rt_more.at[1]))
    pl.when(~from_even)(lambda: right(f_odd, rt_more.at[1]))

    @pl.when(group == jnp.where(x == 1, 0, groups - 1))
    def _():
        rt_more[1] = jnp.zeros(rt_more.shape[1:], BF16)

    lefts, lefts_yn = (lh, ll), (lh_yn, ll_yn)
    mid[...] = mid_in[...] + mul(lefts, 1, rt_more, 0) + mul(lefts_yn, 0, rt, 1)
    side[x] = side_in[x]
    side[1 - x] = side_in[1 - x] + mul(lefts, 0, rt_more, 0)

    @pl.when(x == y)
    def _():
        side[y] += mul(lefts_yn, 0, rt_more, 0)

    @pl.when(x != y)
    def _():
        side[1 - x] += mul(lefts, 1, rt_more, 1)


def far_body(f_dg, g_dg, mid_in, side_in, lh, ll, rt, lh_yn, ll_yn, rt_more, mid, side, rt_far, lh_far, ll_far):
    _, _, x, y = place()
    left(g_dg, lh_far.at[0], ll_far.at[0])
    right(f_dg, rt_far.at[0])
    lefts, lefts_yn, lefts_far = (lh, ll), (lh_yn, ll_yn), (lh_far, ll_far)
    mid[...] = mid_in[...] + mul(lefts_far, 0, rt_far, 0)
    side[x] = side_in[x] + mul(lefts_far, 0, rt, 1)
    side[1 - x] = side_in[1 - x] + mul(lefts_yn, 0, rt_far, 0)

    @pl.when(x == y)
    def _():
        side[1 - x] += mul(lefts_far, 0, rt_more, 1)

    @pl.when(x != y)
    def _():
        side[1 - y] += mul(lefts, 0, rt_far, 0)
        side[y] += mul(lefts_far, 0, rt, 0)


def edge_body(groups, owned, g_even, g_odd, mid, side_in, rt_more, rt_far, *refs):
    outs, odds, evens, side, lh, ll = refs[:-5], *refs[-5:]
    group, _, x, y = place()
    n_out = g_even.shape[0]
    from_even = group % 2 == x
    pl.when(from_even)(lambda: left(g_even, lh.at[0], ll.at[0]))
    pl.when(~from_even)(lambda: left(g_odd, lh.at[0], ll.at[0]))

    @pl.when(group == jnp.where(x == 1, 0, groups - 1))
    def _():
        lh[...] = jnp.zeros_like(lh)
        ll[...] = jnp.zeros_like(ll)

    side[1 - x] = side_in[1 - x]

    @pl.when(x == y)
    def _():
        side[x] = side_in[x] + mul((lh, ll), 0, rt_far, 0)

    @pl.when(x != y)
    def _():
        side[x] = side_in[x] + mul((lh, ll), 0, rt_more, 0)

    rows = 2 * owned
    for m in range(groups):
        start = pl.multiple_of((group ^ m) * rows, rows)
        across = (odds if m % 2 else evens).at[m // 2]
        for a, sums in enumerate((side.at[0], mid, side.at[1])):
            for b in range(3):
                both = sums[pl.ds(b * n_out + start, rows), :]
                low, high = both[:owned], both[owned:]
                outs[m][3 * a + b] = jnp.where(y == 0, low, high)
                across[3 * a + b] = jnp.where(y == 0, high, low)


def pair_body(*refs):
    mine, theirs, outs = refs[0], refs[1], refs[2:]
    for k, out in enumerate(outs):
        out[...] = mine[k] + theirs[k]


def sum_body(groups, *refs):
    parts, out = refs[:-1], refs[-1]
    taps = parts[0].shape[0]
    for d, terms in enumerate((parts[:groups], parts[groups:])):
        for t in range(taps):
            total = terms[0][t]
            for term in terms[1:]:
                total = total + term[t]
            out[0, d * taps + t] = total


def final_body(sums_ref, every_ref, mixed_ref, scale_ref, out_ref, held, sem):
    _, _, _, y = place()
    samples, taps = sums_ref.shape[0], sums_ref.shape[1] // 2
    kinds = held.shape[0]
    grads = []
    for s in range(samples):
        pieces = []
        for t in range(taps):
            kept, got = sums_ref[s, t], sums_ref[s, taps + t]
            pieces += [jnp.where(y == 0, kept, got), jnp.where(y == 0, got, kept)]
        grad = jnp.concatenate(pieces, axis=1)
        mixed, scale = mixed_ref[s], scale_ref[s, :, 0:1]
        inner = jnp.sum(mixed * grad, axis=1, keepdims=True)
        grads.append(scale * grad - (scale * scale * scale * inner) * mixed)
    copies = []
    for k in range(kinds):
        total = every_ref[0, k : k + 1, 0:1] * grads[0]
        for s in range(1, samples):
            total = total + every_ref[s, k : k + 1, 0:1] * grads[s]
        held[k] = total
        copies.append(pltpu.make_async_copy(held.at[k], out_ref.at[k], sem.at[k]))
        copies[-1].start()
    for copy in copies:
        copy.wait()


def send(value, pairs, axes="wide"):
    return lax.ppermute(value, axes, pairs)


def local(features, out_grad, bank, mix_seed, style_of):
    size = lax.axis_size("wide")
    groups = size // 4
    _, _, map_width, in_channels = features.shape
    out_channels = out_grad.shape[3]
    owned = bank.shape[1]
    half_in, half_out = in_channels // 2, out_channels // 2
    everyone = range(size)
    over_x = [(i, i ^ 1) for i in everyone]
    over_y = [(i, i ^ 2) for i in everyone]
    cores = lax.axis_size("narrow")
    even = [(i, i ^ 4) for i in everyone]
    odd = []
    for i in everyone:
        group, member = i // 4, i % 4
        other = (group - 1 ^ 1) + 1
        for c in range(cores):
            at_edge = other in (0, groups + 1) or not 0 <= other < groups
            to = (i, c ^ 1) if at_edge else (4 * other + member, c)
            odd.append((i * cores + c, to[0] * cores + to[1]))

    def shape(*dims, dtype=F32):
        return jax.ShapeDtypeStruct(dims, dtype)

    f_shape, g_shape = shape(map_width, half_in), shape(half_out, map_width)
    mix_shape = shape(owned, 128)
    f_keep, f_send = call(features_body, (f_shape, f_shape), "v", flops=2 * 10**9)(features)
    g_keep, g_send = call(functools.partial(grads_body, owned), (g_shape, g_shape), "v")(out_grad)
    mix = call(weights_body, mix_shape, "ssa")(mix_seed.T, style_of, g_send)

    f_yn = send(f_send, over_y)
    g_xn = send(g_send, over_x)
    every_mix = lax.all_gather(mix[None], "narrow", axis=0, tiled=True)
    samples = every_mix.shape[0]
    mixed, scale, f_keep, g_keep = call(
        mix_body,
        (shape(samples, *bank.shape[1:]), shape(samples, owned, 128), f_shape, g_shape),
        "vvaa",
        (VMEM_SPEC, VMEM_SPEC, ANY_SPEC, ANY_SPEC),
        alias={2: 2, 3: 3},
    )(every_mix, bank, f_keep, g_keep)
    f_xn = send(f_keep, over_x)
    g_yn = send(g_keep, over_y)
    f_dg = send(f_yn, over_x)
    g_dg = send(g_xn, over_y)
    me = lax.axis_index("wide")
    same = (me % 2) == ((me // 2) % 2)
    f_out = jnp.where(same, f_keep, f_yn)
    g_out = jnp.where(same, g_keep, g_yn)
    both = ("wide", "narrow")
    f_even = send(f_out, even)
    f_odd = send(f_out, odd, both)
    g_even = send(g_out, even)
    g_odd = send(g_out, odd, both)

    pair = 2 * 3 * 3 * half_out * half_in * map_width
    mids = shape(3 * half_out, half_in)
    sides = shape(2, *mids.shape)

    def lefts(count):
        return shape(count, 3 * half_out, map_width, dtype=BF16)

    def rights(count):
        return shape(count, map_width, 2 * half_in, dtype=BF16)

    mid, side, lh, ll, rt = call(
        first_body, (mids, sides, lefts(2), lefts(2), rights(2)), "vvvv", flops=3 * pair
    )(f_keep, f_yn, g_keep, g_xn)
    mid, side, *more = call(
        functools.partial(near_body, groups),
        (mids, sides, lefts(1), lefts(1), rights(2)),
        "v" * 9,
        flops=4 * pair,
    )(f_xn, g_yn, f_even, f_odd, mid, side, lh, ll, rt)
    mid, side, rt_far = call(
        far_body,
        (mids, sides, rights(1)),
        "v" * 10,
        flops=5 * pair,
        scratch=[pltpu.VMEM(lefts(1).shape, BF16)] * 2,
    )(f_dg, g_dg, mid, side, lh, ll, rt, *more)
    piece = shape(9, owned, half_in)
    stack = shape(groups // 2, *piece.shape)
    *blocks, odds, evens = call(
        functools.partial(edge_body, groups, owned),
        [piece] * groups + [stack] * 2,
        "v" * 6,
        flops=pair,
        scratch=[
            pltpu.VMEM(sides.shape, F32),
            pltpu.VMEM(lefts(1).shape, BF16),
            pltpu.VMEM(lefts(1).shape, BF16),
        ],
    )(g_even, g_odd, mid, side, more[2], rt_far)

    def hop(m, d):
        return [(i, i ^ (4 * m + 2 * d)) for i in everyone]

    theirs = send(odds, hop(1, 0))
    parts = [blocks[0]] + [send(blocks[m], hop(m, 0)) for m in range(1, groups)]
    pairs = call(pair_body, [piece] * (groups // 2), "vv")(evens, theirs)
    parts += [send(pairs[k], hop(2 * k, 1)) for k in range(groups // 2)]
    own_sums = call(
        functools.partial(sum_body, groups), shape(1, 18, owned, half_in), "v" * len(parts)
    )(*parts)
    every_sum = lax.all_gather(own_sums, "narrow", axis=0, tiled=True)
    return call(
        final_body,
        shape(*bank.shape),
        "vvvv",
        ANY_SPEC,
        scratch=(pltpu.VMEM(bank.shape, F32), pltpu.SemaphoreType.DMA((bank.shape[0],))),
    )(every_sum, every_mix, mixed, scale)


def solution(mesh):
    placed = (
        P("narrow", "wide", None, None),
        P("narrow", "wide", None, None),
        P(None, "wide", None),
        P(),
        P("narrow"),
    )
    return jax.shard_map(
        local, mesh=mesh, in_specs=placed, out_specs=P(None, "wide", None), check_vma=False
    )
```

```python
import functools

import jax
import jax.numpy as jnp
from jax import lax
from jax.experimental import pallas as pl
from jax.experimental.pallas import tpu as pltpu
from jax.sharding import PartitionSpec as P


F32, BF16 = jnp.float32, jnp.bfloat16
VMEM_SPEC = pl.BlockSpec(memory_space=pltpu.VMEM)
SMEM_SPEC = pl.BlockSpec(memory_space=pltpu.SMEM)
ANY_SPEC = pl.BlockSpec(memory_space=pl.ANY)


def place():
    me = lax.axis_index("wide")
    return me // 4, me % 4, me % 2, (me // 2) % 2


def call(body, outs, ins, out_specs=None, flops=0, scratch=(), alias=None, limit=40 * 2**20):
    return pl.pallas_call(
        body,
        out_shape=outs,
        in_specs=[{"v": VMEM_SPEC, "s": SMEM_SPEC, "a": ANY_SPEC}[i] for i in ins],
        out_specs=jax.tree.map(lambda _: VMEM_SPEC, outs) if out_specs is None else out_specs,
        scratch_shapes=list(scratch),
        input_output_aliases=alias or {},
        compiler_params=pltpu.CompilerParams(vmem_limit_bytes=limit),
        cost_estimate=pl.CostEstimate(flops=flops, bytes_accessed=2**20, transcendentals=0),
    )


def features_body(f_ref, f_keep, f_send):
    _, _, _, y = place()
    half = f_keep.shape[1]
    f_send[...] = f_ref[0, 0, :, pl.ds(pl.multiple_of((1 - y) * half, half), half)]
    f_keep[...] = f_ref[0, 0, :, pl.ds(pl.multiple_of(y * half, half), half)]


def weights_body(seed_ref, style_ref, after_ref, mix):
    at = lax.broadcasted_iota(jnp.int32, mix.shape, 0)
    tile = jnp.zeros(mix.shape, F32)
    for k in range(seed_ref.shape[0]):
        weight = seed_ref[k, style_ref[0]].astype(F32) / 128.0 + 0.25
        tile = jnp.where(at == k, weight, tile)
    mix[...] = tile


def grads_body(owned, g_ref, g_keep, g_send):
    _, _, x, _ = place()
    turned = jnp.transpose(g_ref[0, 0])
    for k in range(turned.shape[0] // (2 * owned)):
        low = turned[2 * k * owned : (2 * k + 1) * owned]
        high = turned[(2 * k + 1) * owned : (2 * k + 2) * owned]
        rows = slice(k * owned, (k + 1) * owned)
        g_keep[rows] = jnp.where(x == 0, low, high)
        g_send[rows] = jnp.where(x == 0, high, low)


def mix_body(every_ref, bank_ref, mixed_ref, scale_ref):
    samples, kinds = every_ref.shape[0], bank_ref.shape[0]
    for s in range(samples):
        mixed = every_ref[s, 0:1, 0:1] * bank_ref[0]
        for k in range(1, kinds):
            mixed = mixed + every_ref[s, k : k + 1, 0:1] * bank_ref[k]
        mixed_ref[s] = mixed
        scale = lax.rsqrt(jnp.sum(mixed * mixed, axis=1, keepdims=True) + 1e-08)
        scale_ref[s] = jnp.broadcast_to(scale, scale_ref.shape[1:])


def split(v):
    high = v.astype(BF16)
    return high, (v - high.astype(F32)).astype(BF16)


def shifted(g):
    width = g.shape[1]
    at = lax.broadcasted_iota(jnp.int32, g.shape, 1)
    ahead = jnp.where(at == width - 1, 0.0, pltpu.roll(g, width - 1, 1))
    behind = jnp.where(at == 0, 0.0, pltpu.roll(g, 1, 1))
    return split(jnp.concatenate([ahead, g, behind], axis=0))


def product(left_high, left_low, right, half):
    both = jnp.dot(left_high, right, preferred_element_type=F32)
    return (
        both[:, :half]
        + both[:, half:]
        + jnp.dot(left_low, right[:, :half], preferred_element_type=F32)
    )


def left(g, high, low):
    high[...], low[...] = shifted(g[...])


def right(f, out):
    half = f.shape[1]
    high, low = split(f[...])
    out[:, :half] = high
    out[:, half:] = low


def mul(lefts, role, rights, other):
    half = rights.shape[2] // 2
    return product(lefts[0][role], lefts[1][role], rights[other], half)


def first_body(f_own, f_yn, g_own, g_xn, mid, side, lh, ll, rt):
    _, _, x, y = place()
    left(g_own, lh.at[0], ll.at[0])
    left(g_xn, lh.at[1], ll.at[1])
    right(f_own, rt.at[0])
    right(f_yn, rt.at[1])
    lefts = (lh, ll)
    mid[...] = mul(lefts, 0, rt, 0)
    side[x] = mul(lefts, 1, rt, 0)
    side[1 - x] = jnp.zeros(side.shape[1:], F32)

    @pl.when(x == y)
    def _():
        side[1 - y] += mul(lefts, 1, rt, 1)


def near_body(groups, f_xn, g_yn, f_even, f_odd, mid_in, side_in, lh, ll, rt, mid, side, lh_yn, ll_yn, rt_more):
    group, _, x, y = place()
    left(g_yn, lh_yn.at[0], ll_yn.at[0])
    right(f_xn, rt_more.at[0])
    from_even = group % 2 == x
    pl.when(from_even)(lambda: right(f_even, rt_more.at[1]))
    pl.when(~from_even)(lambda: right(f_odd, rt_more.at[1]))

    @pl.when(group == jnp.where(x == 1, 0, groups - 1))
    def _():
        rt_more[1] = jnp.zeros(rt_more.shape[1:], BF16)

    lefts, lefts_yn = (lh, ll), (lh_yn, ll_yn)
    mid[...] = mid_in[...] + mul(lefts, 1, rt_more, 0) + mul(lefts_yn, 0, rt, 1)
    side[x] = side_in[x]
    side[1 - x] = side_in[1 - x] + mul(lefts, 0, rt_more, 0)

    @pl.when(x == y)
    def _():
        side[y] += mul(lefts_yn, 0, rt_more, 0)

    @pl.when(x != y)
    def _():
        side[1 - x] += mul(lefts, 1, rt_more, 1)


def far_body(f_dg, g_dg, mid_in, side_in, lh, ll, rt, lh_yn, ll_yn, rt_more, mid, side, rt_far, lh_far, ll_far):
    _, _, x, y = place()
    left(g_dg, lh_far.at[0], ll_far.at[0])
    right(f_dg, rt_far.at[0])
    lefts, lefts_yn, lefts_far = (lh, ll), (lh_yn, ll_yn), (lh_far, ll_far)
    mid[...] = mid_in[...] + mul(lefts_far, 0, rt_far, 0)
    side[x] = side_in[x] + mul(lefts_far, 0, rt, 1)
    side[1 - x] = side_in[1 - x] + mul(lefts_yn, 0, rt_far, 0)

    @pl.when(x == y)
    def _():
        side[1 - x] += mul(lefts_far, 0, rt_more, 1)

    @pl.when(x != y)
    def _():
        side[1 - y] += mul(lefts, 0, rt_far, 0)
        side[y] += mul(lefts_far, 0, rt, 0)


def edge_body(groups, owned, g_even, g_odd, mid, side_in, rt_more, rt_far, *refs):
    outs, odds, evens, side, lh, ll = refs[:-5], *refs[-5:]
    group, _, x, y = place()
    n_out = g_even.shape[0]
    from_even = group % 2 == x
    pl.when(from_even)(lambda: left(g_even, lh.at[0], ll.at[0]))
    pl.when(~from_even)(lambda: left(g_odd, lh.at[0], ll.at[0]))

    @pl.when(group == jnp.where(x == 1, 0, groups - 1))
    def _():
        lh[...] = jnp.zeros_like(lh)
        ll[...] = jnp.zeros_like(ll)

    side[1 - x] = side_in[1 - x]

    @pl.when(x == y)
    def _():
        side[x] = side_in[x] + mul((lh, ll), 0, rt_far, 0)

    @pl.when(x != y)
    def _():
        side[x] = side_in[x] + mul((lh, ll), 0, rt_more, 0)

    rows = 2 * owned
    for m in range(groups):
        start = pl.multiple_of((group ^ m) * rows, rows)
        along = (odds if m % 2 else evens).at[m // 2]
        for a, sums in enumerate((side.at[0], mid, side.at[1])):
            for b in range(3):
                both = sums[pl.ds(b * n_out + start, rows), :]
                low, high = both[:owned], both[owned:]
                outs[m][3 * a + b] = jnp.where(y == 0, high, low)
                along[3 * a + b] = jnp.where(y == 0, low, high)


def pair_body(*refs):
    mine, theirs, outs = refs[0], refs[1], refs[2:]
    for k, out in enumerate(outs):
        out[...] = mine[k] + theirs[k]


def sum_body(*refs):
    terms, out = refs[:-1], refs[-1]
    for t in range(out.shape[0]):
        total = terms[0][t]
        for term in terms[1:]:
            total = total + term[t]
        out[t] = total


def final_body(kept_own, kept_more, got_own, got_more, every_ref, mixed_ref, scale_ref, out_ref, held, sem):
    _, _, _, y = place()
    samples, taps = every_ref.shape[0], kept_own.shape[0]
    kinds = held.shape[0]
    grads, weights = [], []
    for s in range(samples):
        kept = kept_own if s == 0 else kept_more.at[s - 1]
        got = got_own if s == 0 else got_more.at[s - 1]
        pieces = []
        for t in range(taps):
            pieces += [jnp.where(y == 0, kept[t], got[t]), jnp.where(y == 0, got[t], kept[t])]
        grad = jnp.concatenate(pieces, axis=1)
        mixed, scale = mixed_ref[s], scale_ref[s, :, 0:1]
        inner = jnp.sum(mixed * grad, axis=1, keepdims=True)
        grads.append(scale * grad - (scale * scale * scale * inner) * mixed)
        weights.append(every_ref[s])
    copies = []
    for k in range(kinds):
        total = weights[0][k : k + 1, 0:1] * grads[0]
        for s in range(1, samples):
            total = total + weights[s][k : k + 1, 0:1] * grads[s]
        held[k] = total
        copies.append(pltpu.make_async_copy(held.at[k], out_ref.at[k], sem.at[k]))
        copies[-1].start()
    for copy in copies:
        copy.wait()


def send(value, pairs, axes="wide"):
    return lax.ppermute(value, axes, pairs)


def local(features, out_grad, bank, mix_seed, style_of):
    size = lax.axis_size("wide")
    groups = size // 4
    _, _, map_width, in_channels = features.shape
    out_channels = out_grad.shape[3]
    owned = bank.shape[1]
    half_in, half_out = in_channels // 2, out_channels // 2
    everyone = range(size)
    over_x = [(i, i ^ 1) for i in everyone]
    over_y = [(i, i ^ 2) for i in everyone]
    cores = lax.axis_size("narrow")
    even = [(i, i ^ 4) for i in everyone]
    odd = []
    for i in everyone:
        group, member = i // 4, i % 4
        other = (group - 1 ^ 1) + 1
        for c in range(cores):
            at_edge = other in (0, groups + 1) or not 0 <= other < groups
            to = (i, c ^ 1) if at_edge else (4 * other + member, c)
            odd.append((i * cores + c, to[0] * cores + to[1]))

    def shape(*dims, dtype=F32):
        return jax.ShapeDtypeStruct(dims, dtype)

    f_shape, g_shape = shape(map_width, half_in), shape(half_out, map_width)
    mix_shape = shape(owned, 128)
    f_keep, f_send = call(features_body, (f_shape, f_shape), "v", flops=2 * 10**9)(features)
    g_keep, g_send = call(functools.partial(grads_body, owned), (g_shape, g_shape), "v")(out_grad)
    mix = call(weights_body, mix_shape, "ssa")(mix_seed.T, style_of, g_send)

    f_yn = send(f_send, over_y)
    g_xn = send(g_send, over_x)

    def others(value):
        return [send(value, [((c + s) % cores, c) for c in range(cores)], "narrow") for s in range(1, cores)]

    every_mix = jnp.stack([mix] + others(mix))
    samples = every_mix.shape[0]
    mixed, scale = call(mix_body, (shape(samples, *bank.shape[1:]), shape(samples, owned, 128)), "vv")(every_mix, bank)
    f_xn = send(f_keep, over_x)
    g_yn = send(g_keep, over_y)
    f_dg = send(f_yn, over_x)
    g_dg = send(g_xn, over_y)
    me = lax.axis_index("wide")
    same = (me % 2) == ((me // 2) % 2)
    f_out = jnp.where(same, f_keep, f_yn)
    g_out = jnp.where(same, g_keep, g_yn)
    both = ("wide", "narrow")
    f_even = send(f_out, even)
    f_odd = send(f_out, odd, both)
    g_even = send(g_out, even)
    g_odd = send(g_out, odd, both)

    pair = 2 * 3 * 3 * half_out * half_in * map_width
    mids = shape(3 * half_out, half_in)
    sides = shape(2, *mids.shape)

    def lefts(count):
        return shape(count, 3 * half_out, map_width, dtype=BF16)

    def rights(count):
        return shape(count, map_width, 2 * half_in, dtype=BF16)

    mid, side, lh, ll, rt = call(
        first_body, (mids, sides, lefts(2), lefts(2), rights(2)), "vvvv", flops=3 * pair
    )(f_keep, f_yn, g_keep, g_xn)
    mid, side, *more = call(
        functools.partial(near_body, groups), (mids, sides, lefts(1), lefts(1), rights(2)), "v" * 9, flops=4 * pair
    )(f_xn, g_yn, f_even, f_odd, mid, side, lh, ll, rt)
    mid, side, rt_far = call(
        far_body, (mids, sides, rights(1)), "v" * 10, flops=5 * pair, scratch=[pltpu.VMEM(lefts(1).shape, BF16)] * 2
    )(f_dg, g_dg, mid, side, lh, ll, rt, *more)
    piece = shape(9, owned, half_in)
    stack = shape(groups // 2, *piece.shape)
    *blocks, odds, evens = call(
        functools.partial(edge_body, groups, owned),
        [piece] * groups + [stack] * 2,
        "v" * 6,
        flops=pair,
        scratch=[
            pltpu.VMEM(sides.shape, F32),
            pltpu.VMEM(lefts(1).shape, BF16),
            pltpu.VMEM(lefts(1).shape, BF16),
        ],
    )(g_even, g_odd, mid, side, more[2], rt_far)

    def hop(m, d):
        return [(i, i ^ (4 * m + 2 * d)) for i in everyone]

    theirs = send(odds, hop(1, 0))
    parts = [send(blocks[m], hop(m, 1)) for m in range(groups)]
    pairs = call(pair_body, [piece] * (groups // 2), "vv")(evens, theirs)
    parts += [pairs[0]]
    parts += [send(pairs[k], hop(2 * k, 0)) for k in range(1, groups // 2)]
    got = call(sum_body, piece, "v" * groups)(*parts[:groups])
    kept = call(sum_body, piece, "v" * (groups // 2))(*parts[groups:])

    return call(
        final_body,
        shape(*bank.shape),
        "v" * 7,
        ANY_SPEC,
        scratch=(pltpu.VMEM(bank.shape, F32), pltpu.SemaphoreType.DMA((bank.shape[0],))),
    )(kept, jnp.stack(others(kept)), got, jnp.stack(others(got)), every_mix, mixed, scale)


def solution(mesh):
    placed = (
        P("narrow", "wide", None, None),
        P("narrow", "wide", None, None),
        P(None, "wide", None),
        P(),
        P("narrow"),
    )
    return jax.shard_map(
        local, mesh=mesh, in_specs=placed, out_specs=P(None, "wide", None), check_vma=False
    )
```

```python
import functools

import jax
import jax.numpy as jnp
from jax import lax
from jax.experimental import pallas as pl
from jax.experimental.pallas import tpu as pltpu
from jax.sharding import PartitionSpec as P


F32, BF16 = jnp.float32, jnp.bfloat16
VMEM_SPEC = pl.BlockSpec(memory_space=pltpu.VMEM)
SMEM_SPEC = pl.BlockSpec(memory_space=pltpu.SMEM)
ANY_SPEC = pl.BlockSpec(memory_space=pl.ANY)


def place():
    me = lax.axis_index("wide")
    return me // 4, me % 4, me % 2, (me // 2) % 2


def call(body, outs, ins, out_specs=None, flops=0, scratch=(), alias=None, limit=40 * 2**20):
    return pl.pallas_call(
        body,
        out_shape=outs,
        in_specs=[{"v": VMEM_SPEC, "s": SMEM_SPEC, "a": ANY_SPEC}[i] for i in ins],
        out_specs=jax.tree.map(lambda _: VMEM_SPEC, outs) if out_specs is None else out_specs,
        scratch_shapes=list(scratch),
        input_output_aliases=alias or {},
        compiler_params=pltpu.CompilerParams(vmem_limit_bytes=limit),
        cost_estimate=pl.CostEstimate(flops=flops, bytes_accessed=2**20, transcendentals=0),
    )


def features_body(f_ref, f_keep, f_send):
    _, _, _, y = place()
    half = f_keep.shape[1]
    f_send[...] = f_ref[0, 0, :, pl.ds(pl.multiple_of((1 - y) * half, half), half)]
    f_keep[...] = f_ref[0, 0, :, pl.ds(pl.multiple_of(y * half, half), half)]


def weights_body(seed_ref, style_ref, after_ref, mix):
    at = lax.broadcasted_iota(jnp.int32, mix.shape, 0)
    tile = jnp.zeros(mix.shape, F32)
    for k in range(seed_ref.shape[0]):
        weight = seed_ref[k, style_ref[0]].astype(F32) / 128.0 + 0.25
        tile = jnp.where(at == k, weight, tile)
    mix[...] = tile


def grads_body(owned, g_ref, g_keep, g_send):
    _, _, x, _ = place()
    turned = jnp.transpose(g_ref[0, 0])
    for k in range(turned.shape[0] // (2 * owned)):
        low = turned[2 * k * owned : (2 * k + 1) * owned]
        high = turned[(2 * k + 1) * owned : (2 * k + 2) * owned]
        rows = slice(k * owned, (k + 1) * owned)
        g_keep[rows] = jnp.where(x == 0, low, high)
        g_send[rows] = jnp.where(x == 0, high, low)


def mix_body(every_ref, bank_ref, mixed_ref, scale_ref):
    samples, kinds = every_ref.shape[0], bank_ref.shape[0]
    for s in range(samples):
        mixed = every_ref[s, 0:1, 0:1] * bank_ref[0]
        for k in range(1, kinds):
            mixed = mixed + every_ref[s, k : k + 1, 0:1] * bank_ref[k]
        mixed_ref[s] = mixed
        scale = lax.rsqrt(jnp.sum(mixed * mixed, axis=1, keepdims=True) + 1e-08)
        scale_ref[s] = jnp.broadcast_to(scale, scale_ref.shape[1:])


def split(v):
    high = v.astype(BF16)
    return high, (v - high.astype(F32)).astype(BF16)


def shifted(g):
    width = g.shape[1]
    at = lax.broadcasted_iota(jnp.int32, g.shape, 1)
    ahead = jnp.where(at == width - 1, 0.0, pltpu.roll(g, width - 1, 1))
    behind = jnp.where(at == 0, 0.0, pltpu.roll(g, 1, 1))
    return split(jnp.concatenate([ahead, g, behind], axis=0))


def product(left_high, left_low, right, half):
    both = jnp.dot(left_high, right, preferred_element_type=F32)
    return (
        both[:, :half]
        + both[:, half:]
        + jnp.dot(left_low, right[:, :half], preferred_element_type=F32)
    )


def left(g, high, low):
    high[...], low[...] = shifted(g[...])


def right(f, out):
    half = f.shape[1]
    high, low = split(f[...])
    out[:, :half] = high
    out[:, half:] = low


def mul(lefts, role, rights, other):
    half = rights.shape[2] // 2
    return product(lefts[0][role], lefts[1][role], rights[other], half)


def mul_two(lefts, role, first, second):
    half = first.shape[1] // 2
    high, low = lefts[0][role], lefts[1][role]
    lows = jnp.dot(
        low,
        jnp.concatenate([first[:, :half], second[:, :half]], axis=1),
        preferred_element_type=F32,
    )
    sums = []
    for right_one, rest in ((first, lows[:, :half]), (second, lows[:, half:])):
        both = jnp.dot(high, right_one, preferred_element_type=F32)
        sums.append(both[:, :half] + both[:, half:] + rest)
    return sums


def first_body(f_own, f_yn, g_own, g_xn, mid, side, lh, ll, rt):
    _, _, x, y = place()
    left(g_own, lh.at[0], ll.at[0])
    left(g_xn, lh.at[1], ll.at[1])
    right(f_own, rt.at[0])
    right(f_yn, rt.at[1])
    lefts = (lh, ll)
    mid[...] = mul(lefts, 0, rt, 0)
    side[x] = mul(lefts, 1, rt, 0)
    side[1 - x] = jnp.zeros(side.shape[1:], F32)

    @pl.when(x == y)
    def _():
        side[1 - y] += mul(lefts, 1, rt, 1)


def near_body(groups, f_xn, g_yn, f_even, f_odd, mid_in, side_in, lh, ll, rt, mid, side, lh_yn, ll_yn, rt_more):
    group, _, x, y = place()
    left(g_yn, lh_yn.at[0], ll_yn.at[0])
    right(f_xn, rt_more.at[0])
    from_even = group % 2 == x
    pl.when(from_even)(lambda: right(f_even, rt_more.at[1]))
    pl.when(~from_even)(lambda: right(f_odd, rt_more.at[1]))

    @pl.when(group == jnp.where(x == 1, 0, groups - 1))
    def _():
        rt_more[1] = jnp.zeros(rt_more.shape[1:], BF16)

    lefts, lefts_yn = (lh, ll), (lh_yn, ll_yn)
    mid[...] = mid_in[...] + mul(lefts, 1, rt_more, 0) + mul(lefts_yn, 0, rt, 1)
    side[x] = side_in[x]
    side[1 - x] = side_in[1 - x] + mul(lefts, 0, rt_more, 0)

    @pl.when(x == y)
    def _():
        side[y] += mul(lefts_yn, 0, rt_more, 0)

    @pl.when(x != y)
    def _():
        side[1 - x] += mul(lefts, 1, rt_more, 1)


def far_body(f_dg, g_dg, mid_in, side_in, lh, ll, rt, lh_yn, ll_yn, rt_more, mid, side, rt_far, lh_far, ll_far):
    _, _, x, y = place()
    left(g_dg, lh_far.at[0], ll_far.at[0])
    right(f_dg, rt_far.at[0])
    lefts, lefts_yn, lefts_far = (lh, ll), (lh_yn, ll_yn), (lh_far, ll_far)
    with_far, with_yn = mul_two(lefts_far, 0, rt_far[0], rt[1])
    mid[...] = mid_in[...] + with_far
    side[x] = side_in[x] + with_yn
    side[1 - x] = side_in[1 - x] + mul(lefts_yn, 0, rt_far, 0)

    @pl.when(x == y)
    def _():
        side[1 - x] += mul(lefts_far, 0, rt_more, 1)

    @pl.when(x != y)
    def _():
        side[1 - y] += mul(lefts, 0, rt_far, 0)
        side[y] += mul(lefts_far, 0, rt, 0)


def edge_body(groups, owned, g_even, g_odd, mid, side_in, rt_more, rt_far, *refs):
    outs, odds, evens, side, lh, ll = refs[:-5], *refs[-5:]
    group, _, x, y = place()
    n_out = g_even.shape[0]
    from_even = group % 2 == x
    pl.when(from_even)(lambda: left(g_even, lh.at[0], ll.at[0]))
    pl.when(~from_even)(lambda: left(g_odd, lh.at[0], ll.at[0]))

    @pl.when(group == jnp.where(x == 1, 0, groups - 1))
    def _():
        lh[...] = jnp.zeros_like(lh)
        ll[...] = jnp.zeros_like(ll)

    side[1 - x] = side_in[1 - x]

    @pl.when(x == y)
    def _():
        side[x] = side_in[x] + mul((lh, ll), 0, rt_far, 0)

    @pl.when(x != y)
    def _():
        side[x] = side_in[x] + mul((lh, ll), 0, rt_more, 0)

    rows = 2 * owned
    for m in range(groups):
        start = pl.multiple_of((group ^ m) * rows, rows)
        along = (odds if m % 2 else evens).at[m // 2]
        for a, sums in enumerate((side.at[0], mid, side.at[1])):
            for b in range(3):
                both = sums[pl.ds(b * n_out + start, rows), :]
                low, high = both[:owned], both[owned:]
                outs[m][3 * a + b] = jnp.where(y == 0, high, low)
                along[3 * a + b] = jnp.where(y == 0, low, high)


def pair_body(*refs):
    mine, theirs, outs = refs[0], refs[1], refs[2:]
    for k, out in enumerate(outs):
        out[...] = mine[k] + theirs[k]


def sum_body(*refs):
    terms, out = refs[:-1], refs[-1]
    for t in range(out.shape[0]):
        total = terms[0][t]
        for term in terms[1:]:
            total = total + term[t]
        out[t] = total


def final_body(kept_own, kept_more, got_own, got_more, every_ref, mixed_ref, scale_ref, out_ref, held, sem):
    _, _, _, y = place()
    samples, taps = every_ref.shape[0], kept_own.shape[0]
    kinds = held.shape[0]
    grads, weights = [], []
    for s in range(samples):
        kept = kept_own if s == 0 else kept_more.at[s - 1]
        got = got_own if s == 0 else got_more.at[s - 1]
        pieces = []
        for t in range(taps):
            pieces += [jnp.where(y == 0, kept[t], got[t]), jnp.where(y == 0, got[t], kept[t])]
        grad = jnp.concatenate(pieces, axis=1)
        mixed, scale = mixed_ref[s], scale_ref[s, :, 0:1]
        inner = jnp.sum(mixed * grad, axis=1, keepdims=True)
        grads.append(scale * grad - (scale * scale * scale * inner) * mixed)
        weights.append(every_ref[s])
    copies = []
    for k in range(kinds):
        total = weights[0][k : k + 1, 0:1] * grads[0]
        for s in range(1, samples):
            total = total + weights[s][k : k + 1, 0:1] * grads[s]
        held[k] = total
        copies.append(pltpu.make_async_copy(held.at[k], out_ref.at[k], sem.at[k]))
        copies[-1].start()
    for copy in copies:
        copy.wait()


def send(value, pairs, axes="wide"):
    return lax.ppermute(value, axes, pairs)


def local(features, out_grad, bank, mix_seed, style_of):
    size = lax.axis_size("wide")
    groups = size // 4
    _, _, map_width, in_channels = features.shape
    out_channels = out_grad.shape[3]
    owned = bank.shape[1]
    half_in, half_out = in_channels // 2, out_channels // 2
    everyone = range(size)
    over_x = [(i, i ^ 1) for i in everyone]
    over_y = [(i, i ^ 2) for i in everyone]
    cores = lax.axis_size("narrow")
    even = [(i, i ^ 4) for i in everyone]
    odd = []
    for i in everyone:
        group, member = i // 4, i % 4
        other = (group - 1 ^ 1) + 1
        for c in range(cores):
            at_edge = other in (0, groups + 1) or not 0 <= other < groups
            to = (i, c ^ 1) if at_edge else (4 * other + member, c)
            odd.append((i * cores + c, to[0] * cores + to[1]))

    def shape(*dims, dtype=F32):
        return jax.ShapeDtypeStruct(dims, dtype)

    f_shape, g_shape = shape(map_width, half_in), shape(half_out, map_width)
    mix_shape = shape(owned, 128)
    f_keep, f_send = call(features_body, (f_shape, f_shape), "v", flops=2 * 10**9)(features)
    g_keep, g_send = call(functools.partial(grads_body, owned), (g_shape, g_shape), "v")(out_grad)
    mix = call(weights_body, mix_shape, "ssa")(mix_seed.T, style_of, g_send)

    f_yn = send(f_send, over_y)
    g_xn = send(g_send, over_x)

    def others(value):
        return [
            send(value, [((c + s) % cores, c) for c in range(cores)], "narrow")
            for s in range(1, cores)
        ]

    every_mix = jnp.stack([mix] + others(mix))
    samples = every_mix.shape[0]
    mixed, scale = call(
        mix_body, (shape(samples, *bank.shape[1:]), shape(samples, owned, 128)), "vv"
    )(every_mix, bank)
    f_xn = send(f_keep, over_x)
    g_yn = send(g_keep, over_y)
    f_dg = send(f_yn, over_x)
    g_dg = send(g_xn, over_y)
    me = lax.axis_index("wide")
    same = (me % 2) == ((me // 2) % 2)
    f_out = jnp.where(same, f_keep, f_yn)
    g_out = jnp.where(same, g_keep, g_yn)
    both = ("wide", "narrow")
    f_even = send(f_out, even)
    f_odd = send(f_out, odd, both)
    g_even = send(g_out, even)
    g_odd = send(g_out, odd, both)

    pair = 2 * 3 * 3 * half_out * half_in * map_width
    mids = shape(3 * half_out, half_in)
    sides = shape(2, *mids.shape)

    def lefts(count):
        return shape(count, 3 * half_out, map_width, dtype=BF16)

    def rights(count):
        return shape(count, map_width, 2 * half_in, dtype=BF16)

    mid, side, lh, ll, rt = call(
        first_body, (mids, sides, lefts(2), lefts(2), rights(2)), "vvvv", flops=3 * pair
    )(f_keep, f_yn, g_keep, g_xn)
    mid, side, *more = call(
        functools.partial(near_body, groups),
        (mids, sides, lefts(1), lefts(1), rights(2)),
        "v" * 9,
        flops=4 * pair,
    )(f_xn, g_yn, f_even, f_odd, mid, side, lh, ll, rt)
    mid, side, rt_far = call(
        far_body,
        (mids, sides, rights(1)),
        "v" * 10,
        flops=5 * pair,
        scratch=[pltpu.VMEM(lefts(1).shape, BF16)] * 2,
    )(f_dg, g_dg, mid, side, lh, ll, rt, *more)
    piece = shape(9, owned, half_in)
    stack = shape(groups // 2, *piece.shape)
    *blocks, odds, evens = call(
        functools.partial(edge_body, groups, owned),
        [piece] * groups + [stack] * 2,
        "v" * 6,
        flops=pair,
        scratch=[
            pltpu.VMEM(sides.shape, F32),
            pltpu.VMEM(lefts(1).shape, BF16),
            pltpu.VMEM(lefts(1).shape, BF16),
        ],
    )(g_even, g_odd, mid, side, more[2], rt_far)

    def hop(m, d):
        return [(i, i ^ (4 * m + 2 * d)) for i in everyone]

    theirs = send(odds, hop(1, 0))
    parts = [send(blocks[m], hop(m, 1)) for m in range(groups)]
    pairs = call(pair_body, [piece] * (groups // 2), "vv")(evens, theirs)
    parts += [pairs[0]]
    parts += [send(pairs[k], hop(2 * k, 0)) for k in range(1, groups // 2)]
    got = call(sum_body, piece, "v" * groups)(*parts[:groups])
    kept = call(sum_body, piece, "v" * (groups // 2))(*parts[groups:])

    return call(
        final_body,
        shape(*bank.shape),
        "v" * 7,
        ANY_SPEC,
        scratch=(pltpu.VMEM(bank.shape, F32), pltpu.SemaphoreType.DMA((bank.shape[0],))),
    )(kept, jnp.stack(others(kept)), got, jnp.stack(others(got)), every_mix, mixed, scale)


def solution(mesh):
    placed = (
        P("narrow", "wide", None, None),
        P("narrow", "wide", None, None),
        P(None, "wide", None),
        P(),
        P("narrow"),
    )
    return jax.shard_map(
        local, mesh=mesh, in_specs=placed, out_specs=P(None, "wide", None), check_vma=False
    )
```
